32 devices in a mesh: box: 8 (over z, x), lvl: 4 (over y, core).
Axes of the slice: x: 2, y: 2, z: 4, core: 2. Of those that a mesh axis runs over, the one named last changes fastest.
Arguments:
- near_blocks: bfloat16 [32, 24, 256, 256], P('box', 'lvl'), may hold values from -0.375 to 0.375
- self_block: bfloat16 [32, 256, 256], P('box', 'lvl'), as said below
- basis: bfloat16 [32, 256, 256], P('box', 'lvl'), may hold values from -1.5 to 1.5
- neighbours: int32 [32, 24], P('box', 'lvl'), may hold values from -1 to 31, as said below
- counts: int32 [32], P('box'), may hold values from 128 to 256
Outputs:
- fill_blocks: bfloat16 [32, 24, 128, 256], P('box', 'lvl')
The draws below stay inside these ranges and needn't reach their ends.
Inputs may be any that keep to these rules, and one draw needn't show every extreme that they name: `neighbours`: box i is owned by index i // 4 of box. Each box lists distinct other boxes, all owned by indices at most 3 away from its own owner; slots hold -1 only for boxes owned within 3 indices of either end of the axis, and there only after the used slots run out. `self_block`: Symmetric, with a positive diagonal.
All inputs are finite; a program needn't handle non-finite values.
Results may differ from the reference program's by a relative error of at most 0.007.
Values may be sent and summed in bfloat16 or wider, within the bound.
No kernel may reach another device: no remote copies, remote signals or barrier semaphores. Data moves between devices by JAX's collectives and lax.ppermute only.
A program may use at most 64 MiB of HBM per device.

```python
import jax
import jax.numpy as jnp
from jax import lax

LEAF = 256
RED = 128
NEAR = 24
HOPS = 3
BOX_DEV = 4
BOXES = 32
N_BOX = 8


def draw_self_block(key, part):
    box_count = BOX_DEV * N_BOX
    first_key, second_key = jax.random.split(jax.random.fold_in(key, 7))
    diagonal = jax.random.uniform(first_key, (box_count, LEAF), jnp.float32, 1.0, 4.0)
    noise = jax.random.normal(second_key, (box_count, LEAF, LEAF), jnp.float32) * (0.4 / LEAF ** 0.5)
    symmetric = (noise + jnp.swapaxes(noise, 1, 2)) * 0.5 ** 0.5
    identity = jnp.eye(LEAF, dtype=jnp.float32)
    whole = symmetric * (1.0 - identity) + diagonal[:, :, None] * identity
    return whole.astype(jnp.bfloat16)


def draw_neighbours(key, part):
    box_count = BOX_DEV * N_BOX
    window_size = (2 * HOPS + 1) * BOX_DEV
    box_ids = jnp.arange(box_count, dtype=jnp.int32)
    owner = box_ids // BOX_DEV
    candidate = (owner - HOPS)[:, None] * BOX_DEV + jnp.arange(window_size, dtype=jnp.int32)[None, :]
    usable = (candidate >= 0) & (candidate < box_count) & (candidate != box_ids[:, None])
    scores = jax.random.randint(jax.random.fold_in(key, 11), (box_count, window_size), 0, 2 ** 20, dtype=jnp.int32)
    scores = scores * window_size + jnp.arange(window_size, dtype=jnp.int32)[None, :]
    scores = jnp.where(usable, scores, 2 ** 30)
    ordering = jnp.argsort(scores, axis=1, stable=True)[:, :NEAR]
    picked = jnp.take_along_axis(candidate, ordering, axis=1)
    picked_ok = jnp.take_along_axis(usable, ordering, axis=1)
    return jnp.where(picked_ok, picked, -1).astype(jnp.int32)


def touch_ends(values, own_key, low, largest):
    dims = values.shape
    spot = [jax.random.randint(jax.random.fold_in(own_key, axis), (), 0, dims[axis]) for axis in range(len(dims))]
    values = values.at[tuple(spot)].set(low)
    longest = dims.index(max(dims))
    spot[longest] = (spot[longest] + 1) % dims[longest]
    return values.at[tuple(spot)].set(largest)


def block_scale(key, shape, pieces, smallest, top_value):
    def one(position, shards_of):
        heights = jax.random.uniform(jax.random.fold_in(jax.random.fold_in(key, 6), position), (shards_of,), jnp.float32, smallest / len(pieces), top_value / len(pieces))
        return jnp.repeat(jnp.exp(heights), shape[position] // shards_of).reshape((-1,) + (1,) * (len(shape) - position - 1))

    level = one(*pieces[0])
    for cut in pieces[1:]:
        level = level * one(*cut)
    return level


def centred(stream_key, shape, width, reach, cuts=(), kind=jnp.bfloat16):
    values = width * jax.random.normal(stream_key, shape, jnp.float32)
    if cuts:
        values = values * block_scale(stream_key, shape, cuts, -0.22, 0.18)
    return jnp.clip(values, -reach, reach).astype(kind)


def setup_inputs(seed: int = 0) -> dict:
    streams_of = jax.random.split(jax.random.key(seed), 6)
    near_blocks = centred(streams_of[0], (BOXES, NEAR, LEAF, LEAF), LEAF ** -0.5, 0.375, ((0, 8), (1, 4)))
    self_block = draw_self_block(jax.random.fold_in(streams_of[5], 71), 0)
    basis = centred(streams_of[2], (BOXES, LEAF, LEAF), (LEAF // 16) ** -0.5, 1.5, ((0, 8), (1, 4)))
    neighbours = draw_neighbours(jax.random.fold_in(streams_of[5], 71), 0)
    counts = touch_ends(jax.random.randint(streams_of[4], (BOXES,), LEAF // 2, LEAF + 1), jax.random.fold_in(streams_of[4], 1), LEAF // 2, LEAF).astype(jnp.int32)
    return {"near_blocks": near_blocks, "self_block": self_block, "basis": basis, "neighbours": neighbours, "counts": counts}


def solve_block(summed):
    corner = summed[:RED, :RED]
    side = summed[RED:, :RED]
    lower = jnp.linalg.cholesky(corner)
    solved = jax.scipy.linalg.cho_solve((lower, True), side.T)
    return solved.T

def reference(near_blocks, self_block, basis, neighbours, counts):
    positions = jnp.arange(LEAF, dtype=jnp.int32)
    keep_cols = positions[None, :] < counts[:, None]
    zero_value = jnp.zeros((), jnp.bfloat16)
    masked_basis = jnp.where(keep_cols[:, :, None], basis, zero_value)
    identity = positions[:, None] == positions[None, :]

    def one_box(inputs):
        blocks, self_rows, own_basis, own_masked, near_ids, keep_own = inputs
        both_kept = keep_own[:, None] & keep_own[None, :]
        diagonal_fill = jnp.where(identity & ~keep_own[:, None], jnp.ones((), jnp.bfloat16), zero_value)
        adjusted = jnp.where(both_kept, self_rows, diagonal_fill)
        product = jnp.dot(adjusted.astype(jnp.float32), own_basis.astype(jnp.float32), preferred_element_type=jnp.float32).astype(jnp.bfloat16)
        summed = jnp.dot(own_basis.T.astype(jnp.float32), product.astype(jnp.float32), preferred_element_type=jnp.float32)
        factor = solve_block(summed)
        near_basis = masked_basis[jnp.maximum(near_ids, 0)]
        near_work = jnp.einsum('krc,kcs->krs', blocks.astype(jnp.float32), near_basis.astype(jnp.float32))
        near_work = jnp.where(keep_own[None, :, None], near_work, 0.0).astype(jnp.bfloat16)
        projected = jnp.einsum('ck,jcs->jks', own_masked.astype(jnp.float32), near_work.astype(jnp.float32))
        update = jnp.einsum('ij,kjs->kis', factor, projected[:, :RED, :], precision=lax.Precision.HIGHEST)
        result = projected[:, RED:, :] - update
        result = jnp.where((near_ids >= 0)[:, None, None], result, 0.0)
        return result.astype(jnp.bfloat16)
    return lax.map(one_box, (near_blocks, self_block, basis, masked_basis, neighbours, keep_cols))
```

```python
import functools

import jax
import jax.numpy as jnp
from jax import lax
from jax.experimental import pallas as pl
from jax.experimental.pallas import tpu as pltpu
from jax.sharding import PartitionSpec as P

RANK = 128
PAD = 16
NB = 32
AXES = ("box", "lvl")


def move(value, boxes, levels, target):
    pairs = []
    for b in range(boxes):
        for v in range(levels):
            to = target(b, v)
            if to is not None and 0 <= to[0] < boxes:
                pairs.append((b * levels + v, to[0] * levels + to[1]))
    return lax.ppermute(value, AXES, pairs)


def invert_packed(d, nb):
    lanes = lax.broadcasted_iota(jnp.int32, d.shape, 1)
    rows = lax.broadcasted_iota(jnp.int32, d.shape, 0)
    first = lanes // nb * nb
    within = lanes % nb
    group = 4
    for start in range(0, nb, group):
        cols = [jnp.take_along_axis(d, first + (start + q), axis=1) for q in range(group)]
        for q in range(group):
            p = start + q
            col = cols[q]
            inv = 1.0 / col[p : p + 1, :]
            at_row = rows == p
            for later in range(q + 1, group):
                scaled = cols[later][p : p + 1, :] * inv
                cols[later] = jnp.where(at_row, scaled, cols[later] - col * scaled)
            at_lane = within == p
            new_row = jnp.where(at_lane[:1], inv, d[p : p + 1, :] * inv)
            d = jnp.where(at_row, new_row, jnp.where(at_lane, 0.0, d) - col * new_row)
    return d


def solve_kernel(
    counts_ref, own_ref, other_ref, self_a, self_b, self_c, self_d, near_ref,
    out_ref, raw, selfs, near, mat, weights, sems, near_sem,
):
    boxes, slots = near_ref.shape[0], near_ref.shape[1]
    leaf = near_ref.shape[2]
    piece = leaf // 4
    red = leaf - RANK
    hi = jnp.float32
    level = lax.axis_index("lvl")
    y, c = level // 2, level % 2
    fetch_near = [
        pltpu.make_async_copy(near_ref.at[i], near.at[i], near_sem.at[i]) for i in range(boxes)
    ]
    copies = []
    for n, (src, yy, cc) in enumerate(
        ((own_ref.at[0], y, c), (own_ref.at[1], 1 - y, c), (other_ref.at[0], y, 1 - c), (other_ref.at[1], 1 - y, 1 - c))
    ):
        copies.append(pltpu.make_async_copy(src, raw.at[yy * 2 + cc], sems.at[n]))
    for n, (src, yy, cc) in enumerate(
        ((self_a, y, c), (self_b, 1 - y, c), (self_c, y, 1 - c), (self_d, 1 - y, 1 - c))
    ):
        copies.append(pltpu.make_async_copy(src, selfs.at[yy * 2 + cc], sems.at[4 + n]))
    for copy in copies:
        copy.start()
    for copy in fetch_near:
        copy.start()
    for copy in copies:
        copy.wait()

    row_ids = lax.broadcasted_iota(jnp.int32, (leaf, leaf), 0)
    col_ids = lax.broadcasted_iota(jnp.int32, (leaf, leaf), 1)

    def whole(ref, i):
        return jnp.concatenate([ref[v, i * piece : (i + 1) * piece, :] for v in range(4)], axis=0)

    for i in range(boxes):
        count = counts_ref[i]
        basis = whole(raw, i)
        both = (row_ids < count) & (col_ids < count)
        fill = jnp.where((row_ids == col_ids) & (row_ids >= count), 1.0, 0.0)
        adjusted = jnp.where(both, whole(selfs, i).astype(hi), fill).astype(jnp.bfloat16)
        product = jnp.dot(adjusted, basis[:, :red], preferred_element_type=hi).astype(jnp.bfloat16)
        total = lax.dot_general(product, basis, (((0,), (0,)), ((), ())), preferred_element_type=hi)
        corner = total[:, :red]
        mat[i, :, :red] = (corner + corner.T) * 0.5
        mat[i, :, red:] = total[:, red:]

    lanes = lax.broadcasted_iota(jnp.int32, (NB, red), 1)
    eye = jnp.where(
        lax.broadcasted_iota(jnp.int32, (NB, NB), 0) == lax.broadcasted_iota(jnp.int32, (NB, NB), 1), 1.0, 0.0
    )
    for k in range(red // NB):
        lo, up = k * NB, (k + 1) * NB
        packed = jnp.zeros((NB, red), hi)
        for i in range(boxes):
            block = mat[i, lo:up, :red]
            shift = (i * NB - lo) % red
            if shift:
                block = pltpu.roll(block, shift, axis=1)
            packed = jnp.where(lanes // NB == i, block, packed)
        inverse = invert_packed(packed, NB)
        for i in range(boxes):
            mine = inverse if i == 0 else pltpu.roll(inverse, red - i * NB, axis=1)
            start = red if up == red else 0
            rows = mat[i, lo:up, start:]
            scaled = jnp.dot(mine[:, :NB], rows, precision=lax.Precision.HIGHEST, preferred_element_type=hi)
            col = mat[i, :, lo:up]
            parts = [col[lo:up] - eye]
            if lo:
                parts.insert(0, col[:lo])
            if up < red:
                parts.append(col[up:])
            coef = jnp.concatenate(parts, axis=0)
            mat[i, :, start:] = mat[i, :, start:] - jnp.dot(
                coef, scaled, precision=lax.Precision.HIGHEST, preferred_element_type=hi
            )

    keep_rows = lax.broadcasted_iota(jnp.int32, (leaf, RANK), 0)
    for i in range(boxes):
        basis = whole(raw, i)
        solved = mat[i, :, red:]
        high = solved.astype(jnp.bfloat16)
        low = (solved - high.astype(hi)).astype(jnp.bfloat16)
        reds = basis[:, :red]
        update = jnp.dot(reds, high, preferred_element_type=hi) + jnp.dot(reds, low, preferred_element_type=hi)
        weight = jnp.where(keep_rows < counts_ref[i], basis[:, red:].astype(hi) - update, 0.0).T
        high = weight.astype(jnp.bfloat16)
        weights[i, :RANK] = high
        weights[i, RANK:] = (weight - high.astype(hi)).astype(jnp.bfloat16)

    for i in range(boxes):
        fetch_near[i].wait()
        pair = weights[i]

        def step(k, carry):
            both = jnp.dot(pair, near[i, k], preferred_element_type=hi)
            out_ref[i * slots + k] = (both[:RANK] + both[RANK:]).astype(jnp.bfloat16)
            return carry

        lax.fori_loop(0, slots, step, 0)


def solve(counts, own, other, selfs, near):
    boxes, slots, leaf = near.shape[:3]
    any_spec = pl.BlockSpec(memory_space=pl.ANY)
    return pl.pallas_call(
        solve_kernel,
        out_shape=jax.ShapeDtypeStruct((boxes * slots, RANK, leaf), jnp.bfloat16),
        in_specs=[pl.BlockSpec(memory_space=pltpu.SMEM)] + [any_spec] * 7,
        out_specs=pl.BlockSpec(memory_space=pltpu.VMEM),
        scratch_shapes=[
            pltpu.VMEM((4,) + own.shape[1:], jnp.bfloat16),
            pltpu.VMEM((4,) + selfs[0].shape, jnp.bfloat16),
            pltpu.VMEM(near.shape, jnp.bfloat16),
            pltpu.VMEM((boxes, leaf - RANK, leaf), jnp.float32),
            pltpu.VMEM((boxes, 2 * RANK, leaf), jnp.bfloat16),
            pltpu.SemaphoreType.DMA((8,)),
            pltpu.SemaphoreType.DMA((boxes,)),
        ],
        cost_estimate=pl.CostEstimate(flops=8 * 10**9, bytes_accessed=8 * 10**6, transcendentals=0),
        name="solve",
    )(counts, own, other, *selfs, near)


def apply_kernel(ids_ref, half_ref, *refs):
    arrivals, (out_ref, window, half, sems, half_sem) = refs[:16], refs[16:]
    total, leaf = half_ref.shape[0], half_ref.shape[2]
    boxes = ids_ref.shape[0]
    slots = ids_ref.shape[1]
    piece = leaf // 4
    copies = []
    at = 0
    for n, ref in enumerate(arrivals):
        size = ref.shape[0]
        copies.append(pltpu.make_async_copy(ref, window.at[pl.ds(at, size)], sems.at[n]))
        at += size
    per_core = at // 2
    half_copy = pltpu.make_async_copy(half_ref, half, half_sem)
    half_copy.start()
    for copy in copies:
        copy.start()
    half_copy.wait()
    for copy in copies:
        copy.wait()
    level = lax.axis_index("lvl")
    group = lax.axis_index("box")
    y, c = level // 2, level % 2
    row_ids = lax.broadcasted_iota(jnp.int32, (PAD, leaf), 0)
    lane_ids = lax.broadcasted_iota(jnp.int32, (1, leaf), 1)

    def step(s, carry):
        n = ids_ref[s // slots, s % slots]
        used = n >= 0
        n = jnp.where(used, n, group * boxes)
        g, j = n // boxes, n % boxes
        dz = g // 2 - group // 2
        cross = 2 * (g % 2 != group % 2).astype(jnp.int32)
        first = jnp.where(dz == 0, cross, jnp.where(dz == -1, 4 + cross, jnp.where(dz == 1, 8 + cross, 12)))
        rows = pl.ds(pl.multiple_of(j * piece, piece), piece)
        parts = []
        for v in range(4):
            place = first + (v // 2 != y).astype(jnp.int32) + per_core * (v % 2 != c).astype(jnp.int32)
            parts.append(window[place, rows, :])
        near_basis = jnp.concatenate(parts, axis=0)
        tail = window[first, leaf:, :].astype(jnp.float32)
        count = jnp.sum(jnp.where(row_ids == j, tail, 0.0), axis=0, keepdims=True)
        keep = jnp.where(lane_ids.astype(jnp.float32) < count, 1.0, 0.0).astype(jnp.bfloat16)
        result = jnp.dot(half[s] * keep, near_basis, preferred_element_type=jnp.float32)
        out_ref[s // slots, s % slots] = jnp.where(used, result, 0.0).astype(jnp.bfloat16)
        return carry

    lax.fori_loop(0, total, step, 0)


def apply(ids, half, arrivals):
    boxes, slots = ids.shape
    any_spec = pl.BlockSpec(memory_space=pl.ANY)
    items = sum(a.shape[0] for a in arrivals)
    return pl.pallas_call(
        apply_kernel,
        out_shape=jax.ShapeDtypeStruct((boxes, slots) + half.shape[1:], jnp.bfloat16),
        in_specs=[pl.BlockSpec(memory_space=pltpu.SMEM)] + [any_spec] * (1 + len(arrivals)),
        out_specs=pl.BlockSpec(memory_space=pltpu.VMEM),
        scratch_shapes=[
            pltpu.VMEM((items,) + arrivals[0].shape[1:], jnp.bfloat16),
            pltpu.VMEM(half.shape, jnp.bfloat16),
            pltpu.SemaphoreType.DMA((len(arrivals),)),
            pltpu.SemaphoreType.DMA,
        ],
        cost_estimate=pl.CostEstimate(flops=10**9, bytes_accessed=8 * 10**6, transcendentals=0),
        name="apply",
    )(ids, half, *arrivals)


def local(boxes_axis, levels, near_blocks, self_block, basis, neighbours, counts):
    per, piece, leaf = basis.shape
    send = functools.partial(move, boxes=boxes_axis, levels=levels)
    swap_core = lambda v: send(v, target=lambda b, l: (b, l ^ 1))
    swap_y = lambda v: send(v, target=lambda b, l: (b, l ^ 2))
    swap_x = lambda v: send(v, target=lambda b, l: (b ^ 1, l))
    up = lambda v: send(v, target=lambda b, l: (b + 2, l))
    down = lambda v: send(v, target=lambda b, l: (b - 2, l))
    far = lambda v: send(v, target=lambda b, l: (b + 3 if b % 2 else b - 3, l))

    tail = jnp.broadcast_to(jnp.pad(counts, (0, PAD - per))[:, None], (PAD, leaf)).astype(basis.dtype)
    item = jnp.concatenate([basis.reshape(per * piece, leaf), tail], axis=0)[None]
    self_own = self_block.reshape(per * piece, leaf)
    z2 = far(item)
    item_y = swap_y(item)
    self_y = swap_y(self_own)
    own = jnp.concatenate([item, item_y], axis=0)
    x_pair = swap_x(own)
    up_own = up(own)
    down_own = down(own)
    other = swap_core(own)
    self_c = swap_core(self_own)
    self_yc = swap_core(self_y)
    half = solve(counts, own, other, (self_own, self_y, self_c, self_yc), near_blocks)
    up_x = up(x_pair)
    down_x = down(x_pair)
    z2_y = swap_y(z2)
    mine = [own, x_pair, up_own, up_x, down_own, down_x, z2, z2_y]
    theirs = [other] + [swap_core(v) for v in mine[1:]]
    return apply(neighbours, half, mine + theirs)


def solution(mesh):
    boxes_axis, levels = mesh.shape["box"], mesh.shape["lvl"]
    assert boxes_axis % 2 == 0 and levels == 4
    return jax.shard_map(
        functools.partial(local, boxes_axis, levels),
        mesh=mesh,
        in_specs=(
            P("box", "lvl", None, None),
            P("box", "lvl", None),
            P("box", "lvl", None),
            P("box", "lvl"),
            P("box"),
        ),
        out_specs=P("box", "lvl", None, None),
        check_vma=False,
    )
```
